256 devices in a mesh: segment: 4 (over x_hi, core), fsdp: 64 (over z, x_lo, y).
Axes of the slice: x: 4 (x_hi: 2, x_lo: 2; x = x_hi * 2 + x_lo), y: 4, z: 8, core: 2. Of those that a mesh axis runs over, the one named last changes fastest.
Arguments:
- maps: bfloat16 [32, 64, 64, 1280], P('segment', 'fsdp'), may hold values from -6 to 6
- cotangent: bfloat16 [32, 64, 64, 256], P('segment', 'fsdp'), may hold values from -6 to 6
- w_lat: bfloat16 [1280, 256], P('fsdp'), may hold values from -0.15625 to 0.15625
- w_fpn: bfloat16 [2304, 256], P('fsdp'), may hold values from -0.125 to 0.125
- w_rpn: bfloat16 [2304, 256], P('fsdp'), may hold values from -0.125 to 0.125
- channel_norm_gain: float32 [256], replicated, may hold values from 0.5 to 1.5
- channel_norm_bias: float32 [256], replicated, may hold values from -3 to 3
Outputs:
- map_grad: bfloat16 [32, 64, 64, 1280], P('segment', 'fsdp')
- grad_lat: float32 [1280, 256], P('fsdp')
- grad_fpn: float32 [2304, 256], P('fsdp')
- grad_rpn: float32 [2304, 256], P('fsdp')
The draws below stay inside these ranges and needn't reach their ends.
All inputs are finite; a program needn't handle non-finite values.
Results may differ from the reference program's by a relative error of at most 0.018.
Values may be sent and summed in bfloat16 or wider, within the bound.
A program may use at most 64 MiB of HBM per device.

```python
import jax
import jax.numpy as jnp
from jax import lax

D = 1280
C = 256
MAP_ROWS = 64
MAP_COLS = 64
IMAGES = 32


def shard_levels(own_key, dims, cuts, least, largest):
    level = 1.0
    for axis_at, shards_of in cuts:
        heights = jax.random.uniform(jax.random.fold_in(jax.random.fold_in(own_key, 6), axis_at), (shards_of,), jnp.float32, least / len(cuts), largest / len(cuts))
        level = level * jnp.repeat(jnp.exp(heights), dims[axis_at] // shards_of).reshape((-1,) + (1,) * (len(dims) - 1 - axis_at))
    return level


def scatter_about(key, shape, deviation, most, cuts=(), dtype=jnp.bfloat16):
    drawn = jax.random.normal(key, shape, jnp.float32) * deviation
    if len(cuts) > 0:
        drawn = shard_levels(key, shape, cuts, -0.22, 0.18) * drawn
    return jnp.clip(drawn, min=-most, max=most).astype(dtype)


def setup_inputs(seed: int = 0) -> dict:
    arg_keys = jax.random.split(jax.random.key(seed), 8)
    return {
        "maps": scatter_about(arg_keys[0], (IMAGES, MAP_ROWS, MAP_COLS, D), 1.0, 6.0, ((0, 4), (1, 64))),
        "cotangent": scatter_about(arg_keys[1], (IMAGES, MAP_ROWS, MAP_COLS, C), 1.0, 6.0, ((0, 4), (1, 64))),
        "w_lat": scatter_about(arg_keys[2], (D, C), D ** -0.5, 0.15625, ((0, 64),)),
        "w_fpn": scatter_about(arg_keys[3], (9 * C, C), (9 * C) ** -0.5, 0.125, ((0, 64),)),
        "w_rpn": scatter_about(arg_keys[4], (9 * C, C), (9 * C) ** -0.5, 0.125, ((0, 64),)),
        "channel_norm_gain": jnp.clip(1.0 + 0.1 * jax.random.normal(arg_keys[5], (C,), jnp.float32), 0.5, 1.5),
        "channel_norm_bias": scatter_about(arg_keys[6], (C,), 0.5, 3.0, (), jnp.float32),
    }


def patches(field):
    row_count, column_count = (field.shape[0], field.shape[1])
    padded = jnp.pad(field, ((1, 1), (1, 1), (0, 0)))
    return jnp.concatenate([padded[a:a + row_count, b:b + column_count] for a in range(3) for b in range(3)], axis=-1)

def flipped(weight):
    channel_count = weight.shape[1]
    return weight.reshape(9, channel_count, channel_count)[::-1].transpose(0, 2, 1).reshape(9 * channel_count, channel_count)

def flatten(field):
    return field.reshape(-1, field.shape[-1])

def gelu_tanh(value):
    return jax.nn.gelu(value, approximate=True)

def one_image(image, target, w_lat, w_fpn, w_rpn, channel_norm_gain, channel_norm_bias):
    row_count, column_count = (image.shape[0], image.shape[1])
    channel_count = w_lat.shape[1]
    flat_img = flatten(image)
    lat = jnp.dot(flat_img, w_lat, preferred_element_type=jnp.float32)
    channel_mean = lax.optimization_barrier(jnp.mean(lat, -1, keepdims=True))
    centered_values = lat - channel_mean
    inverse_deviation = lax.rsqrt(lax.optimization_barrier(jnp.mean(centered_values * centered_values, -1, keepdims=True)) + 1e-06)
    normalized_input = centered_values * inverse_deviation
    normalized_output = (normalized_input * channel_norm_gain + channel_norm_bias).astype(jnp.bfloat16).reshape(row_count, column_count, channel_count)
    norm_patch = flatten(patches(normalized_output))
    fpn = jnp.dot(norm_patch, w_fpn, preferred_element_type=jnp.float32).astype(jnp.bfloat16)
    fpn_patch = flatten(patches(fpn.reshape(row_count, column_count, channel_count)))
    pre = jnp.dot(fpn_patch, w_rpn, preferred_element_type=jnp.float32)
    _, back = jax.vjp(gelu_tanh, pre)
    g_pre = back(flatten(target).astype(jnp.float32))[0].astype(jnp.bfloat16)
    sum_rpn = jnp.dot(fpn_patch.T, g_pre, preferred_element_type=jnp.float32)
    d_fpn = jnp.dot(flatten(patches(g_pre.reshape(row_count, column_count, channel_count))), flipped(w_rpn), preferred_element_type=jnp.float32).astype(jnp.bfloat16)
    sum_fpn = jnp.dot(norm_patch.T, d_fpn, preferred_element_type=jnp.float32)
    d_norm = jnp.dot(flatten(patches(d_fpn.reshape(row_count, column_count, channel_count))), flipped(w_fpn), preferred_element_type=jnp.float32)
    output_gradient = d_norm * channel_norm_gain
    lateral_gradient = (inverse_deviation * (output_gradient - lax.optimization_barrier(jnp.mean(output_gradient, -1, keepdims=True)) - normalized_input * lax.optimization_barrier(jnp.mean(output_gradient * normalized_input, -1, keepdims=True)))).astype(jnp.bfloat16)
    sum_lat = jnp.dot(flat_img.T, lateral_gradient, preferred_element_type=jnp.float32)
    map_grad = jnp.dot(lateral_gradient, w_lat.T, preferred_element_type=jnp.float32).astype(jnp.bfloat16)
    return (map_grad.reshape(row_count, column_count, -1), sum_lat, sum_fpn, sum_rpn)

def reference(maps, cotangent, w_lat, w_fpn, w_rpn, channel_norm_gain, channel_norm_bias):

    def step(carry, item):
        grads, sum_lat, sum_fpn, sum_rpn = one_image(item[0], item[1], w_lat, w_fpn, w_rpn, channel_norm_gain, channel_norm_bias)
        return ((carry[0] + sum_lat, carry[1] + sum_fpn, carry[2] + sum_rpn), grads)
    start = (jnp.zeros((D, C), jnp.float32), jnp.zeros((9 * C, C), jnp.float32), jnp.zeros((9 * C, C), jnp.float32))
    totals, grads = lax.scan(step, start, (maps, cotangent))
    return (grads, totals[0] / IMAGES, totals[1] / IMAGES, totals[2] / IMAGES)
```

```python
import jax
import jax.numpy as jnp
from jax import lax
from jax.experimental import pallas as pl
from jax.experimental.pallas import tpu as pltpu
from jax.sharding import PartitionSpec as P

MESH = pl.DeviceIdType.MESH
F32 = jnp.float32
BF16 = jnp.bfloat16
VM = pl.BlockSpec(memory_space=pltpu.VMEM)
VMEM_LIMIT = 60 * 1024 * 1024

PART_ROWS = (80, 144, 144)
PART_AT = (0, 80, 224)
SHARD_ROWS = (20, 36, 36)
SHARD_AT = (0, 20, 56)
BLOCK = 368


def coords():
    seg = lax.axis_index("segment")
    f = lax.axis_index("fsdp")
    core = lax.rem(seg, 2)
    j = lax.rem(f, 8)
    return core, 2 * lax.div(seg, 2) + lax.div(j, 4), lax.rem(j, 4), lax.div(f, 8)


def dev(core, x, y, z):
    x, y, z = lax.rem(x, 4), lax.rem(y, 4), lax.rem(z, 8)
    return (2 * lax.div(x, 2) + core, 8 * z + 4 * lax.rem(x, 2) + y)


def group_dev(core, x, j, z):
    j = lax.rem(j, 8)
    return (2 * lax.div(x, 2) + core, 8 * z + j)


def meet(peers):
    barrier = pltpu.get_barrier_semaphore()
    for peer in peers:
        pl.semaphore_signal(barrier, inc=1, device_id=peer, device_id_type=MESH)
    pl.semaphore_wait(barrier, len(peers))


def push(src, dst, send_sem, recv_sem, to):
    copy = pltpu.make_async_remote_copy(
        src_ref=src, dst_ref=dst, send_sem=send_sem, recv_sem=recv_sem, device_id=to, device_id_type=MESH
    )
    copy.start()
    return copy


def arrive(ref, sem):
    pltpu.make_async_copy(ref, ref, sem).wait()


def gather_kernel(
    shard, cot, wl, wf, wr, c12,
    stage, s32, asm, blk,
    ysend, yrecv, own_sem, zsend, zrecv, xsend, xrecv, dsend, drecv, csend, crecv, hsend, hrecv, out_sem,
):
    core, x, y, z = coords()
    xl = lax.rem(x, 2)
    j = 4 * xl + y
    half = pl.ds(pl.multiple_of(core * 128, 128), 128)
    other = pl.ds(pl.multiple_of((1 - core) * 128, 128), 128)
    partner = dev(1 - core, x, y, z)
    group = [group_dev(core, x, j + o, z) for o in range(1, 8)]
    z_up, z_down = dev(core, x, y, z + 1), dev(core, x, y, z + 7)
    outs = (wl, wf, wr)
    sent = []
    meet(group + [dev(core, x + 3 - 2 * xl, y, z), z_up, z_down, partner])

    own = pltpu.make_async_copy(shard.at[:, half], stage.at[y], own_sem.at[0])
    own.start()
    for o in range(1, 4):
        sent.append(push(shard.at[:, half], stage.at[y], ysend.at[o], yrecv.at[o], dev(core, x, y + o, z)))
    c_own = pltpu.make_async_copy(cot.at[j], c12.at[2 + j], own_sem.at[1])
    c_own.start()
    for o in range(1, 8):
        sent.append(push(cot.at[lax.rem(j + o, 8)], c12.at[2 + j], csend.at[o], crecv.at[o], group[o - 1]))

    own.wait()
    for o in range(1, 4):
        arrive(stage.at[lax.rem(y + 4 - o, 4)], yrecv.at[o])
    s32[...] = stage[...].astype(F32)
    for yy in range(4):
        for w in range(3):
            n = SHARD_ROWS[w]
            asm[PART_AT[w] + n * yy : PART_AT[w] + n * (yy + 1), :] = s32[yy, SHARD_AT[w] : SHARD_AT[w] + n, :]
    blk[...] = asm[...].astype(BF16)

    def place(w, offset, xb, cols):
        return outs[w].at[lax.rem(z + offset + 8, 8), xb, :, cols]

    locals_ = []

    def handle(w, offset):
        here = place(w, offset, xl, half)
        if offset == 0:
            src = blk.at[pl.ds(PART_AT[w], PART_ROWS[w]), :]
            copy = pltpu.make_async_copy(src, here, out_sem.at[w])
            copy.start()
            locals_.append(copy)
        else:
            src = here
            arrive(here, zrecv.at[w, offset + 4])
        reach_up = -3 if w < 2 else -2
        reach_down = 2 if w < 2 else 3
        if reach_up <= offset <= 0:
            sent.append(push(src, here, zsend.at[w, 0, -offset], zrecv.at[w, offset + 3], z_up))
        if 0 <= offset <= reach_down:
            sent.append(push(src, here, zsend.at[w, 1, offset], zrecv.at[w, offset + 5], z_down))
        k = offset % 8
        parity = lax.rem(z + k, 2)
        sent.append(push(src, here, xsend.at[w, k], xrecv.at[w, k], dev(core, x + 1 + 2 * parity, y, z)))
        sent.append(push(src, here, dsend.at[w, k, 0], drecv.at[w, k, 0], partner))

    def hand_over(w, offset):
        k = offset % 8
        there = place(w, offset, 1 - xl, half)
        arrive(there, xrecv.at[w, k])
        sent.append(push(there, there, dsend.at[w, k, 1], drecv.at[w, k, 1], partner))

    for w in range(3):
        handle(w, 0)
    for step in range(1, 5):
        for w in range(3):
            if step < 4:
                handle(w, -step)
                handle(w, step)
            else:
                handle(w, -4 if w < 2 else 4)
        for w in range(3):
            hand_over(w, 1 - step)
            if step > 1:
                hand_over(w, step - 1)
        if step == 2:
            c_own.wait()
            for o in range(1, 8):
                arrive(c12.at[2 + lax.rem(j + 8 - o, 8)], crecv.at[o])
            sent.append(push(c12.at[pl.ds(8, 2)], c12.at[pl.ds(0, 2)], hsend.at[0], hrecv.at[0], z_up))
            sent.append(push(c12.at[pl.ds(2, 2)], c12.at[pl.ds(10, 2)], hsend.at[1], hrecv.at[1], z_down))
    for w in range(3):
        hand_over(w, -4 if w < 2 else 4)
    for w in range(3):
        for k in range(8):
            arrive(place(w, k, xl, other), drecv.at[w, k, 0])
            arrive(place(w, k, 1 - xl, other), drecv.at[w, k, 1])
    arrive(c12.at[pl.ds(0, 2)], hrecv.at[0])
    arrive(c12.at[pl.ds(10, 2)], hrecv.at[1])
    for copy in locals_:
        copy.wait()
    for copy in sent:
        copy.wait_send()


def gather(shard, cot):
    dma = pltpu.SemaphoreType.DMA
    return pl.pallas_call(
        gather_kernel,
        out_shape=(
            jax.ShapeDtypeStruct((8, 2, 80, 256), BF16),
            jax.ShapeDtypeStruct((8, 2, 144, 256), BF16),
            jax.ShapeDtypeStruct((8, 2, 144, 256), BF16),
            jax.ShapeDtypeStruct((12, 64, 256), BF16),
        ),
        in_specs=[VM] * 2,
        out_specs=[VM] * 4,
        scratch_shapes=[
            pltpu.VMEM((4, 96, 128), BF16),
            pltpu.VMEM((4, 96, 128), F32),
            pltpu.VMEM((BLOCK, 128), F32),
            pltpu.VMEM((BLOCK, 128), BF16),
            dma((4,)), dma((4,)), dma((2,)),
            dma((3, 2, 4)), dma((3, 9)), dma((3, 8)), dma((3, 8)), dma((3, 8, 2)), dma((3, 8, 2)),
            dma((8,)), dma((8,)), dma((2,)), dma((2,)), dma((3,)),
        ],
        compiler_params=pltpu.CompilerParams(collective_id=0, has_side_effects=True, vmem_limit_bytes=VMEM_LIMIT),
        name="weight_gather",
    )(shard, cot)


def to_image_kernel(nrm, n16, own_sem, send, recv, hsend, hrecv):
    core, x, y, z = coords()
    j = 4 * lax.rem(x, 2) + y
    group = [group_dev(core, x, j + o, z) for o in range(1, 8)]
    z_up, z_down = dev(core, x, y, z + 1), dev(core, x, y, z + 7)
    meet(group + [z_up, z_down])
    own = pltpu.make_async_copy(nrm.at[j], n16.at[4 + j], own_sem)
    own.start()
    sent = []
    for o in range(1, 8):
        sent.append(push(nrm.at[lax.rem(j + o, 8)], n16.at[4 + j], send.at[o], recv.at[o], group[o - 1]))
    own.wait()
    for o in range(1, 8):
        arrive(n16.at[4 + lax.rem(j + 8 - o, 8)], recv.at[o])
    sent.append(push(n16.at[pl.ds(8, 4)], n16.at[pl.ds(0, 4)], hsend.at[0], hrecv.at[0], z_up))
    sent.append(push(n16.at[pl.ds(4, 4)], n16.at[pl.ds(12, 4)], hsend.at[1], hrecv.at[1], z_down))
    arrive(n16.at[pl.ds(0, 4)], hrecv.at[0])
    arrive(n16.at[pl.ds(12, 4)], hrecv.at[1])
    for copy in sent:
        copy.wait_send()


def to_image(nrm):
    dma = pltpu.SemaphoreType.DMA
    return pl.pallas_call(
        to_image_kernel,
        out_shape=jax.ShapeDtypeStruct((16, 64, 256), BF16),
        in_specs=[VM],
        out_specs=VM,
        scratch_shapes=[dma, dma((8,)), dma((8,)), dma((2,)), dma((2,))],
        compiler_params=pltpu.CompilerParams(collective_id=1, has_side_effects=True, vmem_limit_bytes=VMEM_LIMIT),
        name="rows_to_image",
    )(nrm)


def to_rows_kernel(field, rows, own_sem, send, recv):
    core, x, y, z = coords()
    j = 4 * lax.rem(x, 2) + y
    group = [group_dev(core, x, j + o, z) for o in range(1, 8)]
    meet(group)
    own = pltpu.make_async_copy(field.at[j], rows.at[j], own_sem)
    own.start()
    sent = []
    for o in range(1, 8):
        sent.append(push(field.at[lax.rem(j + o, 8)], rows.at[j], send.at[o], recv.at[o], group[o - 1]))
    own.wait()
    for o in range(1, 8):
        arrive(rows.at[lax.rem(j + 8 - o, 8)], recv.at[o])
    for copy in sent:
        copy.wait_send()


def to_rows(field):
    dma = pltpu.SemaphoreType.DMA
    return pl.pallas_call(
        to_rows_kernel,
        out_shape=jax.ShapeDtypeStruct((8, 64, 256), BF16),
        in_specs=[VM],
        out_specs=VM,
        scratch_shapes=[dma, dma((8,)), dma((8,))],
        compiler_params=pltpu.CompilerParams(collective_id=2, has_side_effects=True, vmem_limit_bytes=VMEM_LIMIT),
        name="image_to_rows",
    )(field)


def tower_kernel(n16, c12, w_fpn, w_rpn, d_norm, sum_fpn, sum_rpn, n3, f3, g3, d3):
    z = lax.div(lax.axis_index("fsdp"), 8)
    column = lax.broadcasted_iota(jnp.int32, (64, 256), 0)

    def inside(row):
        return jnp.logical_and(row >= 0, row < 64)

    def spread(value, dst, at, row):
        value = jnp.where(inside(row), value, 0.0)
        dst[at, :, 256:512] = value.astype(BF16)
        dst[at, :, 0:256] = jnp.where(column == 0, 0.0, pltpu.roll(value, 1, 0)).astype(BF16)
        dst[at, :, 512:768] = jnp.where(column == 63, 0.0, pltpu.roll(value, 63, 0)).astype(BF16)

    @pl.loop(0, 16)
    def _(q):
        spread(n16[q].astype(F32), n3, q, 8 * z - 4 + q)

    def forward(src, at, rows, w_ref):
        total = None
        for a in range(3):
            part = jnp.dot(
                src[pl.ds(at + a, rows)].reshape(rows * 64, 768),
                w_ref[a * 768 : (a + 1) * 768, :],
                preferred_element_type=F32,
            )
            total = part if total is None else total + part
        return total

    def backward(src, at, rows, w_ref):
        total = None
        for a in range(3):
            for b in range(3):
                t = 8 - (3 * a + b)
                part = lax.dot_general(
                    src[pl.ds(at + a, rows), :, b * 256 : (b + 1) * 256].reshape(rows * 64, 256),
                    w_ref[t * 256 : (t + 1) * 256, :],
                    (((1,), (1,)), ((), ())),
                    preferred_element_type=F32,
                )
                total = part if total is None else total + part
        return total

    @pl.loop(0, 2)
    def _(k):
        fpn = forward(n3, k * 7, 7, w_fpn).astype(BF16).astype(F32)
        for r in range(7):
            spread(fpn[r * 64 : (r + 1) * 64], f3, k * 7 + r, 8 * z - 3 + k * 7 + r)

    @pl.loop(0, 2)
    def _(k):
        pre = forward(f3, k * 6, 6, w_rpn)
        cot = c12[pl.ds(k * 6, 6)].reshape(384, 256).astype(F32)
        scale = 0.7978845608028654
        square = pre * pre
        t = jnp.tanh(scale * pre * (1.0 + 0.044715 * square))
        slope = 0.5 * (1.0 + t) + 0.5 * pre * (1.0 - t * t) * (scale * (1.0 + 0.134145 * square))
        g_pre = (cot * slope).astype(BF16).astype(F32)
        for r in range(6):
            spread(g_pre[r * 64 : (r + 1) * 64], g3, k * 6 + r, 8 * z - 2 + k * 6 + r)

    def weight_sum(src, at, errors, dst):
        @pl.loop(0, 3)
        def _(a):
            dst[a] = lax.dot_general(
                src[pl.ds(at + a, 8)].reshape(512, 768),
                errors,
                (((0,), (0,)), ((), ())),
                preferred_element_type=F32,
            ).astype(BF16)

    weight_sum(f3, 2, g3[2:10, :, 256:512].reshape(512, 256), sum_rpn)

    @pl.loop(0, 2)
    def _(k):
        d_fpn = backward(g3, k * 5, 5, w_rpn).astype(BF16).astype(F32)
        for r in range(5):
            spread(d_fpn[r * 64 : (r + 1) * 64], d3, k * 5 + r, 8 * z - 1 + k * 5 + r)

    weight_sum(n3, 3, d3[1:9, :, 256:512].reshape(512, 256), sum_fpn)

    @pl.loop(0, 2)
    def _(k):
        d_norm[pl.ds(k * 4, 4)] = backward(d3, k * 4, 4, w_fpn).astype(BF16).reshape(4, 64, 256)


def tower(n16, c12, w_fpn, w_rpn):
    return pl.pallas_call(
        tower_kernel,
        out_shape=(
            jax.ShapeDtypeStruct((8, 64, 256), BF16),
            jax.ShapeDtypeStruct((3, 768, 256), BF16),
            jax.ShapeDtypeStruct((3, 768, 256), BF16),
        ),
        in_specs=[VM] * 4,
        out_specs=[VM] * 3,
        scratch_shapes=[
            pltpu.VMEM((16, 64, 768), BF16),
            pltpu.VMEM((14, 64, 768), BF16),
            pltpu.VMEM((12, 64, 768), BF16),
            pltpu.VMEM((10, 64, 768), BF16),
        ],
        compiler_params=pltpu.CompilerParams(vmem_limit_bytes=VMEM_LIMIT),
        name="tower",
    )(n16, c12, w_fpn, w_rpn)


ORDER = (4, 3, 5, 2, 6, 1, 7, 0)


def reduce_kernel(
    gl, gf, gr, out,
    ol, of, orr, dl, df, dr, xs, xr, acc, zs, zrf, zrb, fin, p32, pieces, fr, res,
    own_sem, dsend, drecv, xsend, xrecv, fsend, frecv, bsend, brecv, psend, precv, osend, orecv, olocal,
):
    core, x, y, z = coords()
    xl = lax.rem(x, 2)
    half = pl.ds(pl.multiple_of(core * 128, 128), 128)
    other = pl.ds(pl.multiple_of((1 - core) * 128, 128), 128)
    partner = dev(1 - core, x, y, z)
    z_up, z_down = dev(core, x, y, z + 1), dev(core, x, y, z + 7)
    plane = [dev(core, x + 2 * dx, y + dy, z) for dy in range(4) for dx in range(2)]
    meet([partner, dev(core, x + 1, y, z), dev(core, x + 3, y, z), z_up, z_down] + plane[1:])
    given, mine, theirs = (gl, gf, gr), (ol, of, orr), (dl, df, dr)
    sent = []

    def level(k):
        return lax.rem(z + k, 8)

    for k in ORDER:
        for w in range(3):
            sent.append(
                push(given[w].at[level(k), :, :, other], theirs[w].at[level(k)], dsend.at[w, k], drecv.at[w, k], partner)
            )
    copies = [pltpu.make_async_copy(given[w].at[:, :, :, half], mine[w], own_sem.at[w]) for w in range(3)]
    for copy in copies:
        copy.start()
    for copy in copies:
        copy.wait()
    for k in ORDER:
        zb = level(k)
        for w in range(3):
            arrive(theirs[w].at[zb], drecv.at[w, k])
            rows = slice(PART_AT[w], PART_AT[w] + PART_ROWS[w])
            xs[k, rows, :] = (mine[w][zb, 1 - xl].astype(F32) + theirs[w][zb, 1 - xl].astype(F32)).astype(BF16)
        parity = lax.rem(zb, 2)
        sent.append(push(xs.at[k], xr.at[k], xsend.at[k], xrecv.at[k], dev(core, x + 1 + 2 * parity, y, z)))
        for w in range(3):
            rows = slice(PART_AT[w], PART_AT[w] + PART_ROWS[w])
            acc[k, rows, :] = mine[w][zb, xl].astype(F32) + theirs[w][zb, xl].astype(F32)

    cut = (slice(0, 224), slice(224, 368))
    cut_at = (pl.ds(0, 224), pl.ds(224, 144))

    def chain(k, step, part, up):
        value = acc[k, cut[part], :] + xr[k, cut[part], :].astype(F32)
        begins = step == 0 or (step == 1 and (part == 1) == up)
        slots, recv = (zrf, frecv) if up else (zrb, brecv)
        if not begins:
            arrive(slots.at[step - 1, cut_at[part]], recv.at[step - 1, part])
            value = value + slots[step - 1, cut[part], :].astype(F32)
        zs[k, cut[part], :] = value.astype(BF16)
        sent.append(
            push(
                zs.at[k, cut_at[part]],
                slots.at[step, cut_at[part]],
                (fsend if up else bsend).at[step, part],
                recv.at[step, part],
                z_up if up else z_down,
            )
        )

    arrive(xr.at[4], xrecv.at[4])
    chain(4, 0, 0, True)
    chain(4, 0, 1, False)
    for step in range(1, 4):
        arrive(xr.at[4 - step], xrecv.at[4 - step])
        arrive(xr.at[4 + step], xrecv.at[4 + step])
        for part in range(2):
            chain(4 - step, step, part, True)
            chain(4 + step, step, part, False)
    arrive(xr.at[0], xrecv.at[0])
    for part in range(2):
        arrive(zrf.at[3, cut_at[part]], frecv.at[3, part])
        arrive(zrb.at[3, cut_at[part]], brecv.at[3, part])
    fin[...] = acc[0] + xr[0].astype(F32) + zrf[3].astype(F32) + zrb[3].astype(F32)
    for yy in range(4):
        p32[yy, 88:96, :] = jnp.zeros((8, 128), F32)
        for w in range(3):
            n = SHARD_ROWS[w]
            p32[yy, SHARD_AT[w] : SHARD_AT[w] + n, :] = fin[PART_AT[w] + n * yy : PART_AT[w] + n * (yy + 1), :]
    pieces[...] = p32[...].astype(BF16)
    for slot in range(1, 8):
        sent.append(
            push(
                pieces.at[lax.rem(y + slot // 2, 4)], fr.at[slot], psend.at[slot], precv.at[slot], plane[slot]
            )
        )
    total = p32[y]
    for slot in range(1, 8):
        arrive(fr.at[slot], precv.at[slot])
        total = total + fr[slot].astype(F32)
    res[...] = total * (1.0 / 32.0)
    local = pltpu.make_async_copy(res, out.at[:, half], olocal)
    local.start()
    sent.append(push(res, out.at[:, half], osend, orecv, partner))
    arrive(out.at[:, other], orecv)
    local.wait()
    for copy in sent:
        copy.wait_send()


def reduce_all(gl, gf, gr):
    dma = pltpu.SemaphoreType.DMA
    return pl.pallas_call(
        reduce_kernel,
        out_shape=jax.ShapeDtypeStruct((96, 256), F32),
        in_specs=[VM] * 3,
        out_specs=VM,
        scratch_shapes=[
            pltpu.VMEM((8, 2, 80, 128), BF16),
            pltpu.VMEM((8, 2, 144, 128), BF16),
            pltpu.VMEM((8, 2, 144, 128), BF16),
            pltpu.VMEM((8, 2, 80, 128), BF16),
            pltpu.VMEM((8, 2, 144, 128), BF16),
            pltpu.VMEM((8, 2, 144, 128), BF16),
            pltpu.VMEM((8, BLOCK, 128), BF16),
            pltpu.VMEM((8, BLOCK, 128), BF16),
            pltpu.VMEM((8, BLOCK, 128), F32),
            pltpu.VMEM((8, BLOCK, 128), BF16),
            pltpu.VMEM((4, BLOCK, 128), BF16),
            pltpu.VMEM((4, BLOCK, 128), BF16),
            pltpu.VMEM((BLOCK, 128), F32),
            pltpu.VMEM((4, 96, 128), F32),
            pltpu.VMEM((4, 96, 128), BF16),
            pltpu.VMEM((8, 96, 128), BF16),
            pltpu.VMEM((96, 128), F32),
            dma((3,)), dma((3, 8)), dma((3, 8)), dma((8,)), dma((8,)),
            dma((4, 2)), dma((4, 2)), dma((4, 2)), dma((4, 2)), dma((8,)), dma((8,)), dma, dma, dma,
        ],
        compiler_params=pltpu.CompilerParams(collective_id=3, has_side_effects=True, vmem_limit_bytes=VMEM_LIMIT),
        name="grad_reduce",
    )(gl, gf, gr)


def on_device(maps, cotangent, w_lat, w_fpn, w_rpn, gain, bias):
    shard = jnp.pad(jnp.concatenate([w_lat, w_fpn, w_rpn], axis=0), ((0, 4), (0, 0)))
    full_lat, full_fpn, full_rpn, c12 = gather(shard, cotangent.reshape(8, 64, 256))
    full_lat = full_lat.reshape(1280, 256)
    flat = maps.reshape(512, 1280)
    lat = jnp.dot(flat, full_lat, preferred_element_type=F32)
    centered = lat - jnp.mean(lat, -1, keepdims=True)
    inverse = lax.rsqrt(jnp.mean(centered * centered, -1, keepdims=True) + 1e-06)
    xhat = centered * inverse
    normed = (xhat * gain + bias).astype(BF16).reshape(8, 64, 256)
    n16 = to_image(normed)
    d_field, sum_fpn, sum_rpn = tower(n16, c12, full_fpn.reshape(2304, 256), full_rpn.reshape(2304, 256))
    d_norm = to_rows(d_field).reshape(512, 256).astype(F32)
    dy = d_norm * gain
    d_lat = (
        inverse * (dy - jnp.mean(dy, -1, keepdims=True) - xhat * jnp.mean(dy * xhat, -1, keepdims=True))
    ).astype(BF16)
    map_grad = lax.dot_general(
        d_lat, full_lat, (((1,), (1,)), ((), ())), preferred_element_type=F32
    ).astype(BF16)
    sum_lat = lax.dot_general(
        flat, d_lat, (((0,), (0,)), ((), ())), preferred_element_type=F32
    ).astype(BF16)
    grads = reduce_all(
        sum_lat.reshape(8, 2, 80, 256), sum_fpn.reshape(8, 2, 144, 256), sum_rpn.reshape(8, 2, 144, 256)
    )
    return (map_grad.reshape(maps.shape), grads[0:20], grads[20:56], grads[56:92])


def solution(mesh):
    placed = (
        P("segment", "fsdp", None, None),
        P("segment", "fsdp", None, None),
        P("fsdp", None),
        P("fsdp", None),
        P("fsdp", None),
        P(),
        P(),
    )
    return jax.shard_map(
        on_device,
        mesh=mesh,
        in_specs=placed,
        out_specs=(
            P("segment", "fsdp", None, None),
            P("fsdp", None),
            P("fsdp", None),
            P("fsdp", None),
        ),
        check_vma=False,
    )
```

```python
import jax
import jax.numpy as jnp
from jax import lax
from jax.experimental import pallas as pl
from jax.experimental.pallas import tpu as pltpu
from jax.sharding import PartitionSpec as P

MESH = pl.DeviceIdType.MESH
F32 = jnp.float32
BF16 = jnp.bfloat16
VM = pl.BlockSpec(memory_space=pltpu.VMEM)
ANY = pl.BlockSpec(memory_space=pl.ANY)
VMEM_LIMIT = 60 * 1024 * 1024

PART_ROWS = (80, 144, 144)
PART_AT = (0, 80, 224)
SHARD_ROWS = (20, 36, 36)
SHARD_AT = (0, 20, 56)
BLOCK = 368
FAR_FIRST = (4, 3, 5, 2, 6, 1, 7)


def coords():
    seg = lax.axis_index("segment")
    f = lax.axis_index("fsdp")
    core = lax.rem(seg, 2)
    j = lax.rem(f, 8)
    return core, 2 * lax.div(seg, 2) + lax.div(j, 4), lax.rem(j, 4), lax.div(f, 8)


def dev(core, x, y, z):
    x, y, z = lax.rem(x, 4), lax.rem(y, 4), lax.rem(z, 8)
    return (2 * lax.div(x, 2) + core, 8 * z + 4 * lax.rem(x, 2) + y)


def group_dev(core, x, j, z):
    return (2 * lax.div(x, 2) + core, 8 * z + lax.rem(j, 8))


def meet(peers):
    barrier = pltpu.get_barrier_semaphore()
    for peer in peers:
        pl.semaphore_signal(barrier, inc=1, device_id=peer, device_id_type=MESH)
    pl.semaphore_wait(barrier, len(peers))


def arrive(ref, sem):
    pltpu.make_async_copy(ref, ref, sem).wait()


def step_kernel(
    maps_in, cot, shard, gain, bias,
    dlat, wl, grads,
    maps, wf, wr, c12, stage, s32, asm, blk, nrm, n16, xh, iv, n3, f3, g3, d3, dn, back,
    sl, sf, sr, tl, tf, tr, xsl, xsf, xsr, xrl, xrf, xrr, accl, accf, accr,
    zsl, zrl, zsf, zsr, upf, upr, downf, downr, fin, p32, pieces, fr, res,
    local, ysend, yrecv, lsend, lrecv, zsend, zrecv, xsend, xrecv, dsend, drecv, csend, crecv, hsend, hrecv,
    asend, arecv, bsend, brecv, gsend, grecv, gxsend, gxrecv, glsend, glrecv, upsend, uprecv, downsend, downrecv,
    psend, precv, osend, orecv,
):
    core, x, y, z = coords()
    xl = lax.rem(x, 2)
    j = 4 * xl + y
    half = pl.ds(pl.multiple_of(core * 128, 128), 128)
    other = pl.ds(pl.multiple_of((1 - core) * 128, 128), 128)
    partner = dev(1 - core, x, y, z)
    group = [None] + [group_dev(core, x, j + o, z) for o in range(1, 8)]
    column = [None] + [dev(core, x, y, z + o) for o in range(1, 8)]
    plane = [dev(core, x + 2 * dx, y + dy, z) for dy in range(4) for dx in range(2)]
    across = [plane[2 * dy + 1] for dy in range(4)]
    z_up, z_down = column[1], column[7]
    weights = (wl, wf, wr)
    sent = []

    def push(src, dst, send_sem, recv_sem, to):
        copy = pltpu.make_async_remote_copy(
            src_ref=src, dst_ref=dst, send_sem=send_sem, recv_sem=recv_sem, device_id=to, device_id_type=MESH
        )
        copy.start()
        sent.append(copy)

    def keep(src, dst, sem):
        copy = pltpu.make_async_copy(src, dst, sem)
        copy.start()
        return copy

    def level(k):
        return lax.rem(z + k, 8)

    def block_rows(w, k, xb):
        n = PART_ROWS[w]
        return pl.ds(pl.multiple_of((2 * level(k) + xb) * n, 16), n)

    def level_rows(w, k):
        n = 2 * PART_ROWS[w]
        return pl.ds(pl.multiple_of(level(k) * n, 16), n)

    def x_side(k):
        return dev(core, x + 1 + 2 * lax.rem(z + k, 2), y, z)

    maps_copy = keep(maps_in, maps, local.at[0])
    shard_copy = keep(shard.at[:, half], stage.at[y], local.at[1])
    cot_copy = keep(cot.at[j], c12.at[2 + j], local.at[2])
    meet(group[1:] + column[1:] + across + [dev(core, x + 3 - 2 * xl, y, z), partner])

    for o in range(1, 4):
        push(shard.at[:, half], stage.at[y], ysend.at[o], yrecv.at[o], dev(core, x, y + o, z))
    shard_copy.wait()
    for o in range(1, 4):
        arrive(stage.at[lax.rem(y + 4 - o, 4)], yrecv.at[o])
    s32[...] = stage[...].astype(F32)
    for yy in range(4):
        for w in range(3):
            n = SHARD_ROWS[w]
            asm[PART_AT[w] + n * yy : PART_AT[w] + n * (yy + 1), :] = s32[yy, SHARD_AT[w] : SHARD_AT[w] + n, :]
    blk[...] = asm[...].astype(BF16)

    def own_block(w):
        return blk.at[pl.ds(PART_AT[w], PART_ROWS[w]), :]

    def place(w, k, xb):
        return weights[w].at[block_rows(w, k, xb), half]

    for o in FAR_FIRST:
        push(own_block(0), place(0, 0, xl), lsend.at[o], lrecv.at[o], column[o])
    own_copies = [keep(own_block(w), place(w, 0, xl), local.at[3 + w]) for w in range(3)]
    push(own_block(0), place(0, 0, xl), xsend.at[0, 0], xrecv.at[0, 0], x_side(0))

    def take(k):
        here = place(0, k, xl)
        arrive(here, lrecv.at[8 - k])
        push(here, here, xsend.at[0, k], xrecv.at[0, k], x_side(k))

    def relay(w, offset):
        k = offset % 8
        here = place(w, k, xl)
        if offset == 0:
            src = own_block(w)
        else:
            src = here
            arrive(here, zrecv.at[w - 1, offset + 4])
        reach_up = -3 if w == 1 else -2
        reach_down = 2 if w == 1 else 3
        if reach_up <= offset <= 0:
            push(src, here, zsend.at[w - 1, 0, -offset], zrecv.at[w - 1, offset + 3], z_up)
        if 0 <= offset <= reach_down:
            push(src, here, zsend.at[w - 1, 1, offset], zrecv.at[w - 1, offset + 5], z_down)
        push(src, here, xsend.at[w, k], xrecv.at[w, k], x_side(k))

    def hand_over(w, k):
        arrive(place(w, k, 1 - xl), xrecv.at[w, k])
        rows = weights[w].at[level_rows(w, k), half]
        push(rows, rows, dsend.at[w, k], drecv.at[w, k], partner)

    def handed(w):
        for k in range(8):
            arrive(weights[w].at[level_rows(w, k), other], drecv.at[w, k])

    relay(1, 0)
    relay(2, 0)
    for o in range(1, 8):
        push(cot.at[lax.rem(j + o, 8)], c12.at[2 + j], csend.at[o], crecv.at[o], group[o])
    take(7)
    take(1)
    for offset in (-1, 1):
        relay(1, offset)
        relay(2, offset)
    for k in (6, 2, 5, 3, 4):
        take(k)
    for copy in own_copies:
        copy.wait()
    for k in (0, 7, 1):
        hand_over(0, k)
    for offset in (-2, 2):
        relay(1, offset)
        relay(2, offset)
    for k in (6, 2, 5, 3, 4):
        hand_over(0, k)
    cot_copy.wait()
    for o in range(1, 8):
        arrive(c12.at[2 + lax.rem(j + 8 - o, 8)], crecv.at[o])
    push(c12.at[pl.ds(8, 2)], c12.at[pl.ds(0, 2)], hsend.at[0], hrecv.at[0], z_up)
    push(c12.at[pl.ds(2, 2)], c12.at[pl.ds(10, 2)], hsend.at[1], hrecv.at[1], z_down)
    handed(0)
    maps_copy.wait()

    for c in range(2):
        at = [lax.rem(j + 4 * c + 1 + i, 8) for i in range(4)]
        lat = jnp.dot(
            jnp.concatenate([maps[i] for i in at], axis=0), wl[...], preferred_element_type=F32
        )
        for i in range(4):
            value = lat[64 * i : 64 * (i + 1)]
            centered = value - jnp.mean(value, -1, keepdims=True)
            inverse = lax.rsqrt(jnp.mean(centered * centered, -1, keepdims=True) + 1e-06)
            xhat = centered * inverse
            xh[at[i]] = xhat
            iv[at[i]] = jnp.broadcast_to(inverse, (64, 128))
            nrm[at[i]] = (xhat * gain[...] + bias[...]).astype(BF16)
        for i in range(4):
            o = (4 * c + 1 + i) % 8
            if o:
                push(nrm.at[at[i]], n16.at[4 + j], asend.at[o], arecv.at[o], group[o])
            else:
                nrm_copy = keep(nrm.at[at[i]], n16.at[4 + j], local.at[6])

    for offset in (-3, 3):
        relay(1, offset)
        relay(2, offset)
    for k in (0, 7, 1, 6, 2):
        hand_over(1, k)
        hand_over(2, k)
    nrm_copy.wait()
    for o in range(1, 8):
        arrive(n16.at[4 + lax.rem(j + 8 - o, 8)], arecv.at[o])
    push(n16.at[pl.ds(8, 4)], n16.at[pl.ds(0, 4)], hsend.at[2], hrecv.at[2], z_up)
    push(n16.at[pl.ds(4, 4)], n16.at[pl.ds(12, 4)], hsend.at[3], hrecv.at[3], z_down)

    cell = lax.broadcasted_iota(jnp.int32, (64, 256), 0)

    def spread(value, dst, at, row):
        value = jnp.where(jnp.logical_and(row >= 0, row < 64), value, 0.0)
        dst[at, :, 256:512] = value.astype(BF16)
        dst[at, :, 0:256] = jnp.where(cell == 0, 0.0, pltpu.roll(value, 1, 0)).astype(BF16)
        dst[at, :, 512:768] = jnp.where(cell == 63, 0.0, pltpu.roll(value, 63, 0)).astype(BF16)

    def spread_rows(first, last):
        @pl.loop(first, last)
        def _(q):
            spread(n16[q].astype(F32), n3, q, 8 * z - 4 + q)

    spread_rows(4, 12)
    relay(1, -4)
    relay(2, 4)
    for k in (5, 3):
        hand_over(1, k)
        hand_over(2, k)
    hand_over(1, 4)
    hand_over(2, 4)
    arrive(n16.at[pl.ds(0, 4)], hrecv.at[2])
    arrive(n16.at[pl.ds(12, 4)], hrecv.at[3])
    spread_rows(0, 4)
    spread_rows(12, 16)
    handed(1)

    def forward(src, at, rows, w_ref):
        total = None
        for a in range(3):
            part = jnp.dot(
                src[pl.ds(at + a, rows)].reshape(rows * 64, 768),
                w_ref[a * 768 : (a + 1) * 768, :],
                preferred_element_type=F32,
            )
            total = part if total is None else total + part
        return total

    def backward(src, at, rows, w_ref):
        total = None
        for a in range(3):
            for b in range(3):
                t = 8 - (3 * a + b)
                part = lax.dot_general(
                    src[pl.ds(at + a, rows), :, b * 256 : (b + 1) * 256].reshape(rows * 64, 256),
                    w_ref[t * 256 : (t + 1) * 256, :],
                    (((1,), (1,)), ((), ())),
                    preferred_element_type=F32,
                )
                total = part if total is None else total + part
        return total

    @pl.loop(0, 2)
    def _(k):
        fpn = forward(n3, k * 7, 7, wf).astype(BF16).astype(F32)
        for r in range(7):
            spread(fpn[r * 64 : (r + 1) * 64], f3, k * 7 + r, 8 * z - 3 + k * 7 + r)

    handed(2)
    arrive(c12.at[pl.ds(0, 2)], hrecv.at[0])
    arrive(c12.at[pl.ds(10, 2)], hrecv.at[1])

    @pl.loop(0, 2)
    def _(k):
        pre = forward(f3, k * 6, 6, wr)
        cotangent = c12[pl.ds(k * 6, 6)].reshape(384, 256).astype(F32)
        scale = 0.7978845608028654
        square = pre * pre
        t = jnp.tanh(scale * pre * (1.0 + 0.044715 * square))
        slope = 0.5 * (1.0 + t) + 0.5 * pre * (1.0 - t * t) * (scale * (1.0 + 0.134145 * square))
        g_pre = (cotangent * slope).astype(BF16).astype(F32)
        for r in range(6):
            spread(g_pre[r * 64 : (r + 1) * 64], g3, k * 6 + r, 8 * z - 2 + k * 6 + r)

    def weight_sum(src, at, errors, dst):
        for a in range(3):
            value = lax.dot_general(
                src[at + a : at + a + 8].reshape(512, 768),
                errors,
                (((0,), (0,)), ((), ())),
                preferred_element_type=F32,
            ).astype(BF16)
            dst[0, a * 768 : (a + 1) * 768, :] = value[:, :128]
            dst[1, a * 768 : (a + 1) * 768, :] = value[:, 128:]

    sums, theirs = (sl, sf, sr), (tl, tf, tr)
    xs, xr, acc = (xsl, xsf, xsr), (xrl, xrf, xrr), (accl, accf, accr)

    def swap_half(w):
        push(sums[w].at[1 - core], theirs[w], gsend.at[w], grecv.at[w], partner)

    def x_step(w):
        arrive(theirs[w], grecv.at[w])
        for k in FAR_FIRST + (0,):
            rows = block_rows(w, k, 1 - xl)
            xs[w][k] = (sums[w][core, rows, :].astype(F32) + theirs[w][rows, :].astype(F32)).astype(BF16)
            push(xs[w].at[k], xr[w].at[k], gxsend.at[w, k], gxrecv.at[w, k], x_side(k))
        for k in FAR_FIRST + (0,):
            rows = block_rows(w, k, xl)
            acc[w][k] = sums[w][core, rows, :].astype(F32) + theirs[w][rows, :].astype(F32)

    weight_sum(f3, 2, g3[2:10, :, 256:512].reshape(512, 256), sr)
    swap_half(2)

    @pl.loop(0, 2)
    def _(k):
        d_fpn = backward(g3, k * 5, 5, wr).astype(BF16).astype(F32)
        for r in range(5):
            spread(d_fpn[r * 64 : (r + 1) * 64], d3, k * 5 + r, 8 * z - 1 + k * 5 + r)

    x_step(2)

    @pl.loop(0, 2)
    def _(k):
        dn[pl.ds(k * 4, 4)] = backward(d3, k * 4, 4, wf).astype(BF16).reshape(4, 64, 256)

    dn_copy = keep(dn.at[j], back.at[j], local.at[7])
    for o in range(1, 8):
        push(dn.at[lax.rem(j + o, 8)], back.at[j], bsend.at[o], brecv.at[o], group[o])
    weight_sum(n3, 3, d3[1:9, :, 256:512].reshape(512, 256), sf)
    swap_half(1)

    zs, ups, downs = (None, zsf, zsr), (None, upf, upr), (None, downf, downr)

    def chain(w, step, up):
        k = 4 - step if up else 4 + step
        slots, send, recv = (ups[w], upsend, uprecv) if up else (downs[w], downsend, downrecv)
        value = acc[w][k] + xr[w][k].astype(F32)
        if not (step == 0 or (step == 1 and (w == 1) == up)):
            arrive(slots.at[step - 1], recv.at[w - 1, step - 1])
            value = value + slots[step - 1].astype(F32)
        zs[w][k] = value.astype(BF16)
        push(zs[w].at[k], slots.at[step], send.at[w - 1, step], recv.at[w - 1, step], z_up if up else z_down)

    def chain_step(w, step):
        if step == 0:
            arrive(xr[w].at[4], gxrecv.at[w, 4])
            chain(w, 0, w == 2)
            return
        for up in (True, False):
            k = 4 - step if up else 4 + step
            arrive(xr[w].at[k], gxrecv.at[w, k])
            chain(w, step, up)

    chain_step(2, 0)
    x_step(1)
    chain_step(2, 1)

    dn_copy.wait()
    for o in range(1, 8):
        arrive(back.at[lax.rem(j + 8 - o, 8)], brecv.at[o])

    @pl.loop(0, 8)
    def _(i):
        xhat = xh[i]
        dy = back[i].astype(F32) * gain[...]
        inner = dy - jnp.mean(dy, -1, keepdims=True) - xhat * jnp.mean(dy * xhat, -1, keepdims=True)
        inverse = iv[i]
        dlat[i] = (jnp.concatenate([inverse, inverse], axis=1) * inner).astype(BF16)

    errors = dlat[...].reshape(512, 256)
    for c in range(5):
        value = lax.dot_general(
            maps[:, :, c * 256 : (c + 1) * 256].reshape(512, 256),
            errors,
            (((0,), (0,)), ((), ())),
            preferred_element_type=F32,
        ).astype(BF16)
        sl[0, c * 256 : (c + 1) * 256, :] = value[:, :128]
        sl[1, c * 256 : (c + 1) * 256, :] = value[:, 128:]
    swap_half(0)
    chain_step(1, 0)
    x_step(0)
    chain_step(2, 2)
    chain_step(1, 1)
    for k in FAR_FIRST:
        arrive(xr[0].at[k], gxrecv.at[0, k])
        zsl[k] = (accl[k] + xrl[k].astype(F32)).astype(BF16)
        push(zsl.at[k], zrl.at[k], glsend.at[k], glrecv.at[k], column[k])
    chain_step(2, 3)
    chain_step(1, 2)
    chain_step(1, 3)

    arrive(xr[0].at[0], gxrecv.at[0, 0])
    total = accl[0] + xrl[0].astype(F32)
    for k in range(1, 8):
        arrive(zrl.at[k], glrecv.at[k])
        total = total + zrl[k].astype(F32)
    fin[0:80, :] = total
    for w in (2, 1):
        arrive(xr[w].at[0], gxrecv.at[w, 0])
        arrive(ups[w].at[3], uprecv.at[w - 1, 3])
        arrive(downs[w].at[3], downrecv.at[w - 1, 3])
        fin[PART_AT[w] : PART_AT[w] + 144, :] = (
            acc[w][0] + xr[w][0].astype(F32) + ups[w][3].astype(F32) + downs[w][3].astype(F32)
        )
    for yy in range(4):
        p32[yy, 88:96, :] = jnp.zeros((8, 128), F32)
        for w in range(3):
            n = SHARD_ROWS[w]
            p32[yy, SHARD_AT[w] : SHARD_AT[w] + n, :] = fin[PART_AT[w] + n * yy : PART_AT[w] + n * (yy + 1), :]
    pieces[...] = p32[...].astype(BF16)
    for slot in range(1, 8):
        push(pieces.at[lax.rem(y + slot // 2, 4)], fr.at[slot], psend.at[slot], precv.at[slot], plane[slot])
    total = p32[y]
    for slot in range(1, 8):
        arrive(fr.at[slot], precv.at[slot])
        total = total + fr[slot].astype(F32)
    res[...] = total * (1.0 / 32.0)
    last = keep(res, grads.at[:, half], local.at[8])
    push(res, grads.at[:, half], osend, orecv, partner)
    arrive(grads.at[:, other], orecv)
    last.wait()
    for copy in sent:
        copy.wait_send()


def one_step(maps, cot, shard, gain, bias):
    dma = pltpu.SemaphoreType.DMA
    vmem = pltpu.VMEM
    return pl.pallas_call(
        step_kernel,
        out_shape=(
            jax.ShapeDtypeStruct((8, 64, 256), BF16),
            jax.ShapeDtypeStruct((1280, 256), BF16),
            jax.ShapeDtypeStruct((96, 256), F32),
        ),
        in_specs=[ANY, ANY, VM, VM, VM],
        out_specs=[VM] * 3,
        scratch_shapes=[
            vmem((8, 64, 1280), BF16),
            vmem((2304, 256), BF16),
            vmem((2304, 256), BF16),
            vmem((12, 64, 256), BF16),
            vmem((4, 96, 128), BF16),
            vmem((4, 96, 128), F32),
            vmem((BLOCK, 128), F32),
            vmem((BLOCK, 128), BF16),
            vmem((8, 64, 256), BF16),
            vmem((16, 64, 256), BF16),
            vmem((8, 64, 256), F32),
            vmem((8, 64, 128), F32),
            vmem((16, 64, 768), BF16),
            vmem((14, 64, 768), BF16),
            vmem((12, 64, 768), BF16),
            vmem((10, 64, 768), BF16),
            vmem((8, 64, 256), BF16),
            vmem((8, 64, 256), BF16),
            vmem((2, 1280, 128), BF16),
            vmem((2, 2304, 128), BF16),
            vmem((2, 2304, 128), BF16),
            vmem((1280, 128), BF16),
            vmem((2304, 128), BF16),
            vmem((2304, 128), BF16),
        ]
        + [vmem((8, n, 128), BF16) for n in PART_ROWS]
        + [vmem((8, n, 128), BF16) for n in PART_ROWS]
        + [vmem((8, n, 128), F32) for n in PART_ROWS]
        + [vmem((8, 80, 128), BF16)] * 2
        + [vmem((8, 144, 128), BF16)] * 2
        + [vmem((4, 144, 128), BF16)] * 4
        + [
            vmem((BLOCK, 128), F32),
            vmem((4, 96, 128), F32),
            vmem((4, 96, 128), BF16),
            vmem((8, 96, 128), BF16),
            vmem((96, 128), F32),
            dma((9,)),
            dma((4,)), dma((4,)),
            dma((8,)), dma((8,)),
            dma((2, 2, 4)), dma((2, 9)),
            dma((3, 8)), dma((3, 8)),
            dma((3, 8)), dma((3, 8)),
            dma((8,)), dma((8,)),
            dma((4,)), dma((4,)),
            dma((8,)), dma((8,)),
            dma((8,)), dma((8,)),
            dma((3,)), dma((3,)),
            dma((3, 8)), dma((3, 8)),
            dma((8,)), dma((8,)),
            dma((2, 4)), dma((2, 4)),
            dma((2, 4)), dma((2, 4)),
            dma((8,)), dma((8,)),
            dma, dma,
        ],
        compiler_params=pltpu.CompilerParams(collective_id=0, has_side_effects=True, vmem_limit_bytes=VMEM_LIMIT),
        name="whole_step",
    )(maps, cot, shard, gain, bias)


def finish_kernel(dlat, wl, grads, map_grad, g_lat, g_fpn, g_rpn):
    for c in range(2):
        map_grad[256 * c : 256 * (c + 1), :] = lax.dot_general(
            dlat[4 * c : 4 * (c + 1)].reshape(256, 256), wl[...], (((1,), (1,)), ((), ())), preferred_element_type=F32
        ).astype(BF16)
    g_lat[...] = grads[0:20, :]
    g_fpn[...] = grads[20:56, :]
    g_rpn[...] = grads[56:92, :]


def finish(dlat, wl, grads):
    return pl.pallas_call(
        finish_kernel,
        out_shape=(
            jax.ShapeDtypeStruct((512, 1280), BF16),
            jax.ShapeDtypeStruct((20, 256), F32),
            jax.ShapeDtypeStruct((36, 256), F32),
            jax.ShapeDtypeStruct((36, 256), F32),
        ),
        in_specs=[VM] * 3,
        out_specs=[VM] * 4,
        compiler_params=pltpu.CompilerParams(vmem_limit_bytes=VMEM_LIMIT),
        name="map_gradient",
    )(dlat, wl, grads)


def on_device(maps, cotangent, w_lat, w_fpn, w_rpn, gain, bias):
    shard = jnp.pad(jnp.concatenate([w_lat, w_fpn, w_rpn], axis=0), ((0, 4), (0, 0)))
    dlat, wl, grads = one_step(
        maps.reshape(8, 64, 1280), cotangent.reshape(8, 64, 256), shard, gain.reshape(1, 256), bias.reshape(1, 256)
    )
    map_grad, g_lat, g_fpn, g_rpn = finish(dlat, wl, grads)
    return (map_grad.reshape(maps.shape), g_lat, g_fpn, g_rpn)


def solution(mesh):
    placed = (
        P("segment", "fsdp", None, None),
        P("segment", "fsdp", None, None),
        P("fsdp", None),
        P("fsdp", None),
        P("fsdp", None),
        P(),
        P(),
    )
    return jax.shard_map(
        on_device,
        mesh=mesh,
        in_specs=placed,
        out_specs=(
            P("segment", "fsdp", None, None),
            P("fsdp", None),
            P("fsdp", None),
            P("fsdp", None),
        ),
        check_vma=False,
    )
```

```python
import jax
import jax.numpy as jnp
from jax import lax
from jax.experimental import pallas as pl
from jax.experimental.pallas import tpu as pltpu
from jax.sharding import PartitionSpec as P

MESH = pl.DeviceIdType.MESH
F32 = jnp.float32
BF16 = jnp.bfloat16
VM = pl.BlockSpec(memory_space=pltpu.VMEM)
ANY = pl.BlockSpec(memory_space=pl.ANY)
VMEM_LIMIT = 60 * 1024 * 1024

PART_ROWS = (80, 144, 144)
PART_AT = (0, 80, 224)
SHARD_ROWS = (20, 36, 36)
SHARD_AT = (0, 20, 56)
BLOCK = 368
FAR_FIRST = (4, 3, 5, 2, 6, 1, 7)


def coords():
    seg = lax.axis_index("segment")
    f = lax.axis_index("fsdp")
    core = lax.rem(seg, 2)
    j = lax.rem(f, 8)
    return core, 2 * lax.div(seg, 2) + lax.div(j, 4), lax.rem(j, 4), lax.div(f, 8)


def dev(core, x, y, z):
    x, y, z = lax.rem(x, 4), lax.rem(y, 4), lax.rem(z, 8)
    return (2 * lax.div(x, 2) + core, 8 * z + 4 * lax.rem(x, 2) + y)


def group_dev(core, x, j, z):
    return (2 * lax.div(x, 2) + core, 8 * z + lax.rem(j, 8))


def meet(peers):
    barrier = pltpu.get_barrier_semaphore()
    for peer in peers:
        pl.semaphore_signal(barrier, inc=1, device_id=peer, device_id_type=MESH)
    pl.semaphore_wait(barrier, len(peers))


def arrive(ref, sem):
    pltpu.make_async_copy(ref, ref, sem).wait()


def step_kernel(
    maps_in, cot, shard, gain, bias,
    dlat, wl, grads,
    maps, wf, wr, c12, stage, s32, asm, blk, nrm, n16, xh, iv, n3, f3, g3, d3, dn, back,
    sl, sf, sr, tl, tf, tr, xsl, xsf, xsr, xrl, xrf, xrr, accl, accf, accr,
    zsl, zrl, zsf, zsr, upf, upr, downf, downr, fin, p32, pieces, fr, res,
    local, ysend, yrecv, lsend, lrecv, zsend, zrecv, xsend, xrecv, dsend, drecv, csend, crecv, hsend, hrecv,
    asend, arecv, bsend, brecv, gsend, grecv, gxsend, gxrecv, glsend, glrecv, upsend, uprecv, downsend, downrecv,
    psend, precv, osend, orecv,
):
    core, x, y, z = coords()
    xl = lax.rem(x, 2)
    j = 4 * xl + y
    half = pl.ds(pl.multiple_of(core * 128, 128), 128)
    other = pl.ds(pl.multiple_of((1 - core) * 128, 128), 128)
    partner = dev(1 - core, x, y, z)
    group = [None] + [group_dev(core, x, j + o, z) for o in range(1, 8)]
    column = [None] + [dev(core, x, y, z + o) for o in range(1, 8)]
    plane = [dev(core, x + 2 * dx, y + dy, z) for dy in range(4) for dx in range(2)]
    across = [plane[2 * dy + 1] for dy in range(4)]
    z_up, z_down = column[1], column[7]
    weights = (wl, wf, wr)
    sent = []

    def push(src, dst, send_sem, recv_sem, to):
        copy = pltpu.make_async_remote_copy(
            src_ref=src, dst_ref=dst, send_sem=send_sem, recv_sem=recv_sem, device_id=to, device_id_type=MESH
        )
        copy.start()
        sent.append(copy)

    def keep(src, dst, sem):
        copy = pltpu.make_async_copy(src, dst, sem)
        copy.start()
        return copy

    def level(k):
        return lax.rem(z + k, 8)

    def block_rows(w, k, xb):
        n = PART_ROWS[w]
        return pl.ds(pl.multiple_of((2 * level(k) + xb) * n, 16), n)

    def level_rows(w, k):
        n = 2 * PART_ROWS[w]
        return pl.ds(pl.multiple_of(level(k) * n, 16), n)

    def x_side(k):
        return dev(core, x + 1 + 2 * lax.rem(z + k, 2), y, z)

    maps_copy = keep(maps_in, maps, local.at[0])
    shard_copy = keep(shard.at[:, half], stage.at[y], local.at[1])
    cot_copy = keep(cot.at[j], c12.at[2 + j], local.at[2])
    meet(group[1:] + column[1:] + across + [dev(core, x + 3 - 2 * xl, y, z), partner])

    for o in range(1, 4):
        push(shard.at[:, half], stage.at[y], ysend.at[o], yrecv.at[o], dev(core, x, y + o, z))
    shard_copy.wait()
    for o in range(1, 4):
        arrive(stage.at[lax.rem(y + 4 - o, 4)], yrecv.at[o])
    s32[...] = stage[...].astype(F32)
    for yy in range(4):
        for w in range(3):
            n = SHARD_ROWS[w]
            asm[PART_AT[w] + n * yy : PART_AT[w] + n * (yy + 1), :] = s32[yy, SHARD_AT[w] : SHARD_AT[w] + n, :]
    blk[...] = asm[...].astype(BF16)

    def own_block(w):
        return blk.at[pl.ds(PART_AT[w], PART_ROWS[w]), :]

    def place(w, k, xb):
        return weights[w].at[block_rows(w, k, xb), half]

    for o in FAR_FIRST:
        push(own_block(0), place(0, 0, xl), lsend.at[o], lrecv.at[o], column[o])
    own_copies = [keep(own_block(w), place(w, 0, xl), local.at[3 + w]) for w in range(3)]
    push(own_block(0), place(0, 0, xl), xsend.at[0, 0], xrecv.at[0, 0], x_side(0))

    def take(k):
        here = place(0, k, xl)
        arrive(here, lrecv.at[8 - k])
        push(here, here, xsend.at[0, k], xrecv.at[0, k], x_side(k))

    def relay(w, offset):
        k = offset % 8
        here = place(w, k, xl)
        if offset == 0:
            src = own_block(w)
        else:
            src = here
            arrive(here, zrecv.at[w - 1, offset + 4])
        reach_up = -3 if w == 1 else -2
        reach_down = 2 if w == 1 else 3
        if reach_up <= offset <= 0:
            push(src, here, zsend.at[w - 1, 0, -offset], zrecv.at[w - 1, offset + 3], z_up)
        if 0 <= offset <= reach_down:
            push(src, here, zsend.at[w - 1, 1, offset], zrecv.at[w - 1, offset + 5], z_down)
        push(src, here, xsend.at[w, k], xrecv.at[w, k], x_side(k))

    def hand_over(w, k):
        arrive(place(w, k, 1 - xl), xrecv.at[w, k])
        rows = weights[w].at[level_rows(w, k), half]
        push(rows, rows, dsend.at[w, k], drecv.at[w, k], partner)

    def handed(w):
        for k in range(8):
            arrive(weights[w].at[level_rows(w, k), other], drecv.at[w, k])

    relay(1, 0)
    relay(2, 0)
    for o in range(1, 8):
        push(cot.at[lax.rem(j + o, 8)], c12.at[2 + j], csend.at[o], crecv.at[o], group[o])
    take(7)
    take(1)
    for offset in (-1, 1):
        relay(1, offset)
        relay(2, offset)
    for k in (6, 2, 5, 3, 4):
        take(k)
    for copy in own_copies:
        copy.wait()
    for k in (0, 7, 1):
        hand_over(0, k)
    for offset in (-2, 2):
        relay(1, offset)
        relay(2, offset)
    for k in (6, 2, 5, 3, 4):
        hand_over(0, k)
    handed(0)
    maps_copy.wait()

    for c in range(2):
        at = [lax.rem(j + 4 * c + 1 + i, 8) for i in range(4)]
        lat = jnp.dot(
            jnp.concatenate([maps[i] for i in at], axis=0), wl[...], preferred_element_type=F32
        )
        for i in range(4):
            value = lat[64 * i : 64 * (i + 1)]
            centered = value - jnp.mean(value, -1, keepdims=True)
            inverse = lax.rsqrt(jnp.mean(centered * centered, -1, keepdims=True) + 1e-06)
            xhat = centered * inverse
            xh[at[i]] = xhat
            iv[at[i]] = jnp.broadcast_to(inverse, (64, 128))
            nrm[at[i]] = (xhat * gain[...] + bias[...]).astype(BF16)
        for i in range(4):
            o = (4 * c + 1 + i) % 8
            if o:
                push(nrm.at[at[i]], n16.at[4 + j], asend.at[o], arecv.at[o], group[o])
            else:
                nrm_copy = keep(nrm.at[at[i]], n16.at[4 + j], local.at[6])

    cot_copy.wait()
    for o in range(1, 8):
        arrive(c12.at[2 + lax.rem(j + 8 - o, 8)], crecv.at[o])
    push(c12.at[pl.ds(8, 2)], c12.at[pl.ds(0, 2)], hsend.at[0], hrecv.at[0], z_up)
    push(c12.at[pl.ds(2, 2)], c12.at[pl.ds(10, 2)], hsend.at[1], hrecv.at[1], z_down)
    for offset in (-3, 3):
        relay(1, offset)
        relay(2, offset)
    for k in (0, 7, 1, 6, 2):
        hand_over(1, k)
        hand_over(2, k)
    nrm_copy.wait()
    for o in range(1, 8):
        arrive(n16.at[4 + lax.rem(j + 8 - o, 8)], arecv.at[o])
    push(n16.at[pl.ds(8, 4)], n16.at[pl.ds(0, 4)], hsend.at[2], hrecv.at[2], z_up)
    push(n16.at[pl.ds(4, 4)], n16.at[pl.ds(12, 4)], hsend.at[3], hrecv.at[3], z_down)

    cell = lax.broadcasted_iota(jnp.int32, (64, 256), 0)

    def spread(value, dst, at, row):
        value = jnp.where(jnp.logical_and(row >= 0, row < 64), value, 0.0)
        dst[at, :, 256:512] = value.astype(BF16)
        dst[at, :, 0:256] = jnp.where(cell == 0, 0.0, pltpu.roll(value, 1, 0)).astype(BF16)
        dst[at, :, 512:768] = jnp.where(cell == 63, 0.0, pltpu.roll(value, 63, 0)).astype(BF16)

    def spread_rows(first, last):
        @pl.loop(first, last)
        def _(q):
            spread(n16[q].astype(F32), n3, q, 8 * z - 4 + q)

    spread_rows(4, 12)
    relay(1, -4)
    relay(2, 4)
    for k in (5, 3):
        hand_over(1, k)
        hand_over(2, k)
    hand_over(1, 4)
    hand_over(2, 4)
    arrive(n16.at[pl.ds(0, 4)], hrecv.at[2])
    arrive(n16.at[pl.ds(12, 4)], hrecv.at[3])
    spread_rows(0, 4)
    spread_rows(12, 16)
    handed(1)

    def forward(src, at, rows, w_ref):
        total = None
        for a in range(3):
            part = jnp.dot(
                src[pl.ds(at + a, rows)].reshape(rows * 64, 768),
                w_ref[a * 768 : (a + 1) * 768, :],
                preferred_element_type=F32,
            )
            total = part if total is None else total + part
        return total

    def backward(src, at, rows, w_ref):
        total = None
        for a in range(3):
            for b in range(3):
                t = 8 - (3 * a + b)
                part = lax.dot_general(
                    src[pl.ds(at + a, rows), :, b * 256 : (b + 1) * 256].reshape(rows * 64, 256),
                    w_ref[t * 256 : (t + 1) * 256, :],
                    (((1,), (1,)), ((), ())),
                    preferred_element_type=F32,
                )
                total = part if total is None else total + part
        return total

    @pl.loop(0, 2)
    def _(k):
        fpn = forward(n3, k * 7, 7, wf).astype(BF16).astype(F32)
        for r in range(7):
            spread(fpn[r * 64 : (r + 1) * 64], f3, k * 7 + r, 8 * z - 3 + k * 7 + r)

    handed(2)
    arrive(c12.at[pl.ds(0, 2)], hrecv.at[0])
    arrive(c12.at[pl.ds(10, 2)], hrecv.at[1])

    @pl.loop(0, 2)
    def _(k):
        pre = forward(f3, k * 6, 6, wr)
        cotangent = c12[pl.ds(k * 6, 6)].reshape(384, 256).astype(F32)
        scale = 0.7978845608028654
        square = pre * pre
        t = jnp.tanh(scale * pre * (1.0 + 0.044715 * square))
        slope = 0.5 * (1.0 + t) + 0.5 * pre * (1.0 - t * t) * (scale * (1.0 + 0.134145 * square))
        g_pre = (cotangent * slope).astype(BF16).astype(F32)
        for r in range(6):
            spread(g_pre[r * 64 : (r + 1) * 64], g3, k * 6 + r, 8 * z - 2 + k * 6 + r)

    def weight_sum(src, at, errors, dst):
        for a in range(3):
            value = lax.dot_general(
                src[at + a : at + a + 8].reshape(512, 768),
                errors,
                (((0,), (0,)), ((), ())),
                preferred_element_type=F32,
            ).astype(BF16)
            dst[0, a * 768 : (a + 1) * 768, :] = value[:, :128]
            dst[1, a * 768 : (a + 1) * 768, :] = value[:, 128:]

    sums, theirs = (sl, sf, sr), (tl, tf, tr)
    xs, xr, acc = (xsl, xsf, xsr), (xrl, xrf, xrr), (accl, accf, accr)

    def swap_half(w):
        push(sums[w].at[1 - core], theirs[w], gsend.at[w], grecv.at[w], partner)

    def x_step(w):
        arrive(theirs[w], grecv.at[w])
        for k in FAR_FIRST + (0,):
            rows = block_rows(w, k, 1 - xl)
            xs[w][k] = (sums[w][core, rows, :].astype(F32) + theirs[w][rows, :].astype(F32)).astype(BF16)
            push(xs[w].at[k], xr[w].at[k], gxsend.at[w, k], gxrecv.at[w, k], x_side(k))
        for k in FAR_FIRST + (0,):
            rows = block_rows(w, k, xl)
            acc[w][k] = sums[w][core, rows, :].astype(F32) + theirs[w][rows, :].astype(F32)

    weight_sum(f3, 2, g3[2:10, :, 256:512].reshape(512, 256), sr)
    swap_half(2)

    @pl.loop(0, 2)
    def _(k):
        d_fpn = backward(g3, k * 5, 5, wr).astype(BF16).astype(F32)
        for r in range(5):
            spread(d_fpn[r * 64 : (r + 1) * 64], d3, k * 5 + r, 8 * z - 1 + k * 5 + r)

    x_step(2)

    @pl.loop(0, 2)
    def _(k):
        dn[pl.ds(k * 4, 4)] = backward(d3, k * 4, 4, wf).astype(BF16).reshape(4, 64, 256)

    dn_copy = keep(dn.at[j], back.at[j], local.at[7])
    for o in range(1, 8):
        push(dn.at[lax.rem(j + o, 8)], back.at[j], bsend.at[o], brecv.at[o], group[o])
    weight_sum(n3, 3, d3[1:9, :, 256:512].reshape(512, 256), sf)
    swap_half(1)

    zs, ups, downs = (None, zsf, zsr), (None, upf, upr), (None, downf, downr)

    def chain(w, step, up):
        k = 4 - step if up else 4 + step
        slots, send, recv = (ups[w], upsend, uprecv) if up else (downs[w], downsend, downrecv)
        value = acc[w][k] + xr[w][k].astype(F32)
        if not (step == 0 or (step == 1 and (w == 1) == up)):
            arrive(slots.at[step - 1], recv.at[w - 1, step - 1])
            value = value + slots[step - 1].astype(F32)
        zs[w][k] = value.astype(BF16)
        push(zs[w].at[k], slots.at[step], send.at[w - 1, step], recv.at[w - 1, step], z_up if up else z_down)

    def chain_step(w, step):
        if step == 0:
            arrive(xr[w].at[4], gxrecv.at[w, 4])
            chain(w, 0, w == 2)
            return
        for up in (True, False):
            k = 4 - step if up else 4 + step
            arrive(xr[w].at[k], gxrecv.at[w, k])
            chain(w, step, up)

    chain_step(2, 0)
    x_step(1)
    chain_step(2, 1)

    dn_copy.wait()
    for o in range(1, 8):
        arrive(back.at[lax.rem(j + 8 - o, 8)], brecv.at[o])

    @pl.loop(0, 8)
    def _(i):
        xhat = xh[i]
        dy = back[i].astype(F32) * gain[...]
        inner = dy - jnp.mean(dy, -1, keepdims=True) - xhat * jnp.mean(dy * xhat, -1, keepdims=True)
        inverse = iv[i]
        dlat[i] = (jnp.concatenate([inverse, inverse], axis=1) * inner).astype(BF16)

    errors = dlat[...].reshape(512, 256)
    for c in range(5):
        value = lax.dot_general(
            maps[:, :, c * 256 : (c + 1) * 256].reshape(512, 256),
            errors,
            (((0,), (0,)), ((), ())),
            preferred_element_type=F32,
        ).astype(BF16)
        sl[0, c * 256 : (c + 1) * 256, :] = value[:, :128]
        sl[1, c * 256 : (c + 1) * 256, :] = value[:, 128:]
    swap_half(0)
    chain_step(1, 0)
    x_step(0)
    chain_step(2, 2)
    chain_step(1, 1)
    for k in FAR_FIRST:
        arrive(xr[0].at[k], gxrecv.at[0, k])
        zsl[k] = (accl[k] + xrl[k].astype(F32)).astype(BF16)
        push(zsl.at[k], zrl.at[k], glsend.at[k], glrecv.at[k], column[k])
    chain_step(2, 3)
    chain_step(1, 2)
    chain_step(1, 3)

    arrive(xr[0].at[0], gxrecv.at[0, 0])
    total = accl[0] + xrl[0].astype(F32)
    for k in range(1, 8):
        arrive(zrl.at[k], glrecv.at[k])
        total = total + zrl[k].astype(F32)
    fin[0:80, :] = total
    for w in (2, 1):
        arrive(xr[w].at[0], gxrecv.at[w, 0])
        arrive(ups[w].at[3], uprecv.at[w - 1, 3])
        arrive(downs[w].at[3], downrecv.at[w - 1, 3])
        fin[PART_AT[w] : PART_AT[w] + 144, :] = (
            acc[w][0] + xr[w][0].astype(F32) + ups[w][3].astype(F32) + downs[w][3].astype(F32)
        )
    for yy in range(4):
        p32[yy, 88:96, :] = jnp.zeros((8, 128), F32)
        for w in range(3):
            n = SHARD_ROWS[w]
            p32[yy, SHARD_AT[w] : SHARD_AT[w] + n, :] = fin[PART_AT[w] + n * yy : PART_AT[w] + n * (yy + 1), :]
    pieces[...] = p32[...].astype(BF16)
    for slot in range(1, 8):
        push(pieces.at[lax.rem(y + slot // 2, 4)], fr.at[slot], psend.at[slot], precv.at[slot], plane[slot])
    total = p32[y]
    for slot in range(1, 8):
        arrive(fr.at[slot], precv.at[slot])
        total = total + fr[slot].astype(F32)
    res[...] = total * (1.0 / 32.0)
    last = keep(res, grads.at[:, half], local.at[8])
    push(res, grads.at[:, half], osend, orecv, partner)
    arrive(grads.at[:, other], orecv)
    last.wait()
    for copy in sent:
        copy.wait_send()


def one_step(maps, cot, shard, gain, bias):
    dma = pltpu.SemaphoreType.DMA
    vmem = pltpu.VMEM
    return pl.pallas_call(
        step_kernel,
        out_shape=(
            jax.ShapeDtypeStruct((8, 64, 256), BF16),
            jax.ShapeDtypeStruct((1280, 256), BF16),
            jax.ShapeDtypeStruct((96, 256), F32),
        ),
        in_specs=[ANY, ANY, VM, VM, VM],
        out_specs=[VM] * 3,
        scratch_shapes=[
            vmem((8, 64, 1280), BF16),
            vmem((2304, 256), BF16),
            vmem((2304, 256), BF16),
            vmem((12, 64, 256), BF16),
            vmem((4, 96, 128), BF16),
            vmem((4, 96, 128), F32),
            vmem((BLOCK, 128), F32),
            vmem((BLOCK, 128), BF16),
            vmem((8, 64, 256), BF16),
            vmem((16, 64, 256), BF16),
            vmem((8, 64, 256), F32),
            vmem((8, 64, 128), F32),
            vmem((16, 64, 768), BF16),
            vmem((14, 64, 768), BF16),
            vmem((12, 64, 768), BF16),
            vmem((10, 64, 768), BF16),
            vmem((8, 64, 256), BF16),
            vmem((8, 64, 256), BF16),
            vmem((2, 1280, 128), BF16),
            vmem((2, 2304, 128), BF16),
            vmem((2, 2304, 128), BF16),
            vmem((1280, 128), BF16),
            vmem((2304, 128), BF16),
            vmem((2304, 128), BF16),
        ]
        + [vmem((8, n, 128), BF16) for n in PART_ROWS]
        + [vmem((8, n, 128), BF16) for n in PART_ROWS]
        + [vmem((8, n, 128), F32) for n in PART_ROWS]
        + [vmem((8, 80, 128), BF16)] * 2
        + [vmem((8, 144, 128), BF16)] * 2
        + [vmem((4, 144, 128), BF16)] * 4
        + [
            vmem((BLOCK, 128), F32),
            vmem((4, 96, 128), F32),
            vmem((4, 96, 128), BF16),
            vmem((8, 96, 128), BF16),
            vmem((96, 128), F32),
            dma((9,)),
            dma((4,)), dma((4,)),
            dma((8,)), dma((8,)),
            dma((2, 2, 4)), dma((2, 9)),
            dma((3, 8)), dma((3, 8)),
            dma((3, 8)), dma((3, 8)),
            dma((8,)), dma((8,)),
            dma((4,)), dma((4,)),
            dma((8,)), dma((8,)),
            dma((8,)), dma((8,)),
            dma((3,)), dma((3,)),
            dma((3, 8)), dma((3, 8)),
            dma((8,)), dma((8,)),
            dma((2, 4)), dma((2, 4)),
            dma((2, 4)), dma((2, 4)),
            dma((8,)), dma((8,)),
            dma, dma,
        ],
        compiler_params=pltpu.CompilerParams(collective_id=0, has_side_effects=True, vmem_limit_bytes=VMEM_LIMIT),
        name="whole_step",
    )(maps, cot, shard, gain, bias)


def finish_kernel(dlat, wl, grads, map_grad, g_lat, g_fpn, g_rpn):
    for c in range(2):
        map_grad[256 * c : 256 * (c + 1), :] = lax.dot_general(
            dlat[4 * c : 4 * (c + 1)].reshape(256, 256), wl[...], (((1,), (1,)), ((), ())), preferred_element_type=F32
        ).astype(BF16)
    g_lat[...] = grads[0:20, :]
    g_fpn[...] = grads[20:56, :]
    g_rpn[...] = grads[56:92, :]


def finish(dlat, wl, grads):
    return pl.pallas_call(
        finish_kernel,
        out_shape=(
            jax.ShapeDtypeStruct((512, 1280), BF16),
            jax.ShapeDtypeStruct((20, 256), F32),
            jax.ShapeDtypeStruct((36, 256), F32),
            jax.ShapeDtypeStruct((36, 256), F32),
        ),
        in_specs=[VM] * 3,
        out_specs=[VM] * 4,
        compiler_params=pltpu.CompilerParams(vmem_limit_bytes=VMEM_LIMIT),
        name="map_gradient",
    )(dlat, wl, grads)


def on_device(maps, cotangent, w_lat, w_fpn, w_rpn, gain, bias):
    shard = jnp.pad(jnp.concatenate([w_lat, w_fpn, w_rpn], axis=0), ((0, 4), (0, 0)))
    dlat, wl, grads = one_step(
        maps.reshape(8, 64, 1280), cotangent.reshape(8, 64, 256), shard, gain.reshape(1, 256), bias.reshape(1, 256)
    )
    map_grad, g_lat, g_fpn, g_rpn = finish(dlat, wl, grads)
    return (map_grad.reshape(maps.shape), g_lat, g_fpn, g_rpn)


def solution(mesh):
    placed = (
        P("segment", "fsdp", None, None),
        P("segment", "fsdp", None, None),
        P("fsdp", None),
        P("fsdp", None),
        P("fsdp", None),
        P(),
        P(),
    )
    return jax.shard_map(
        on_device,
        mesh=mesh,
        in_specs=placed,
        out_specs=(
            P("segment", "fsdp", None, None),
            P("fsdp", None),
            P("fsdp", None),
            P("fsdp", None),
        ),
        check_vma=False,
    )
```
